32 devices in a mesh: section: 2 (over x), dp: 16 (over z, y, core).
Axes of the slice: x: 2, y: 2, z: 4, core: 2. Of those that a mesh axis runs over, the one named last changes fastest.
Arguments:
- block_input: float32 [4096, 1024], P('dp'), may hold values from -6 to 6
- out_grad: float32 [4096, 1024], P('dp'), may hold values from -6 to 6
- in_weight: bfloat16 [2, 1024, 4384], P('section', 'dp'), may hold values from -0.1875 to 0.1875
- out_weight: bfloat16 [2, 1024, 2048], P('section', 'dp'), may hold values from -0.125 to 0.125
- gain_in: float32 [2, 1024], P('section'), may hold values from 0.5 to 1.5
- conv_weight: float32 [2, 4, 2304], P('section'), may hold values from -3 to 3
- conv_bias: float32 [2, 2304], P('section'), may hold values from -3 to 3
- dt_bias: float32 [2, 32], P('section'), may hold values from -5 to -1
- a_log: float32 [2, 32], P('section'), may hold values from -3 to 1
- d_skip: float32 [2, 32], P('section'), may hold values from 0.5 to 1.5
- gain_out: float32 [2, 2048], P('section'), may hold values from 0.5 to 1.5
Outputs:
- activations: float32 [2, 4096, 1024], P('section', 'dp')
- input_grads: float32 [2, 4096, 1024], P('section', 'dp')
- grad_in_weight: float32 [2, 1024, 4384], P('section', 'dp')
- grad_out_weight: float32 [2, 1024, 2048], P('section', 'dp')
- grad_gain_in: float32 [2, 1024], P('section')
- grad_conv_weight: float32 [2, 4, 2304], P('section')
- grad_conv_bias: float32 [2, 2304], P('section')
- grad_dt_bias: float32 [2, 32], P('section')
- grad_a_log: float32 [2, 32], P('section')
- grad_d_skip: float32 [2, 32], P('section')
- grad_gain_out: float32 [2, 2048], P('section')
The draws below stay inside these ranges and needn't reach their ends.
All inputs are finite; a program needn't handle non-finite values.
Results may differ from the reference program's by a relative error of at most 0.009.
Values may be sent and summed in bfloat16 or wider, within the bound.
A program may use at most 256 MiB of HBM per device.

```python
import jax
import jax.numpy as jnp
from jax import lax

D = 1024
DI = 2048
H = 32
P_SIZE = 64
STATE = 128
KCONV = 4
GROUP = 128
LENGTH = 256
CONV = 2304
IN_ALL = 4384
TOKENS = 4096
SEQS = 16


def steps_of(own_key, dims, split, low, high):
    gain = 1.0
    for axis_at, blocks in split:
        heights = jax.random.uniform(jax.random.fold_in(jax.random.fold_in(own_key, 6), axis_at), (blocks,), jnp.float32, low / len(split), high / len(split))
        gain = gain * jnp.repeat(jnp.exp(heights), dims[axis_at] // blocks).reshape((-1,) + (1,) * (len(dims) - 1 - axis_at))
    return gain


def scatter_about(rng, dims, scale, bound, split=(), held_as=jnp.bfloat16):
    array = jax.random.normal(rng, dims, jnp.float32) * scale
    if len(split) > 0:
        array = steps_of(rng, dims, split, -0.22, 0.18) * array
    return jnp.clip(array, min=-bound, max=bound).astype(held_as)


def setup_inputs(seed: int = 0) -> dict:
    splits = jax.random.split(jax.random.key(seed), 12)
    return {
        "block_input": scatter_about(splits[0], (TOKENS, D), 1.0, 6.0, ((0, 16),), jnp.float32),
        "out_grad": scatter_about(splits[1], (TOKENS, D), 1.0, 6.0, ((0, 16),), jnp.float32),
        "in_weight": scatter_about(splits[2], (2, D, IN_ALL), D ** -0.5, 0.1875, ((0, 2), (1, 16))),
        "out_weight": scatter_about(splits[3], (2, D, DI), DI ** -0.5, 0.125, ((0, 2), (1, 16))),
        "gain_in": jnp.clip(0.5 + 1.0 * jax.random.uniform(splits[4], (2, D), jnp.float32) ** steps_of(splits[4], (2, D), ((0, 2),), -0.2, 0.2), 0.5, 1.5),
        "conv_weight": scatter_about(splits[5], (2, KCONV, CONV), KCONV ** -0.5, 3.0, ((0, 2),), jnp.float32),
        "conv_bias": scatter_about(splits[6], (2, CONV), 0.5, 3.0, ((0, 2),), jnp.float32),
        "dt_bias": jnp.clip(-5.0 + 4.0 * jax.random.uniform(splits[7], (2, H), jnp.float32) ** steps_of(splits[7], (2, H), ((0, 2),), -0.2, 0.2), -5.0, -1.0),
        "a_log": jnp.clip(-3.0 + 4.0 * jax.random.uniform(splits[8], (2, H), jnp.float32) ** steps_of(splits[8], (2, H), ((0, 2),), -0.2, 0.2), -3.0, 1.0),
        "d_skip": jnp.clip(0.5 + 1.0 * jax.random.uniform(splits[9], (2, H), jnp.float32) ** steps_of(splits[9], (2, H), ((0, 2),), -0.2, 0.2), 0.5, 1.5),
        "gain_out": jnp.clip(0.5 + 1.0 * jax.random.uniform(splits[10], (2, DI), jnp.float32) ** steps_of(splits[10], (2, DI), ((0, 2),), -0.2, 0.2), 0.5, 1.5),
    }


epsilon = 1e-05
highest = lax.Precision.HIGHEST

def split_conv(projected, halo_rows, conv_weight, conv_bias, dt_bias, a_log):
    row_count = projected.shape[0]
    gate_part = projected[:, :DI]
    raw_part = projected[:, DI:DI + CONV]
    dt_raw = projected[:, DI + CONV:]
    padded = jnp.concatenate([halo_rows, raw_part], axis=0)
    summed = conv_bias[None, :] + conv_weight[0][None, :] * padded[0:row_count]
    for offset in range(1, KCONV):
        summed = summed + conv_weight[offset][None, :] * padded[offset:offset + row_count]
    mixed_rows = jax.nn.silu(summed)
    values = mixed_rows[:, :DI].reshape(row_count, H, P_SIZE)
    b_input = mixed_rows[:, DI:DI + STATE]
    c_output = mixed_rows[:, DI + STATE:]
    step_size = jax.nn.softplus(dt_raw + dt_bias[None, :])
    cumulative = jnp.cumsum(step_size * (-jnp.exp(a_log))[None, :], axis=0)
    return (values, b_input, c_output, step_size, cumulative, gate_part)

def group_state(values, b_input, step_size, cumulative):
    weight = jnp.exp(cumulative[-1:, :] - cumulative) * step_size
    return jnp.einsum('sh,shp,sn->hpn', weight, values, b_input, precision=highest)

def group_output(values, b_input, c_output, step_size, cumulative, gate_part, state_in, d_skip, gain_out):
    row_count = values.shape[0]
    scores = jnp.dot(c_output, b_input.T, precision=highest)
    causal_mask = (jnp.arange(row_count)[:, None] >= jnp.arange(row_count)[None, :])[None, :, :]
    cum_heads = cumulative.T
    log_gap = cum_heads[:, :, None] - cum_heads[:, None, :]
    decays = jnp.where(causal_mask, jnp.exp(jnp.where(causal_mask, log_gap, 0.0)), 0.0)
    mixing = scores[None, :, :] * decays * step_size.T[:, None, :]
    inner_part = jnp.einsum('hts,shp->thp', mixing, values, precision=highest)
    carried = jnp.exp(cumulative)[:, :, None] * jnp.einsum('tn,hpn->thp', c_output, state_in, precision=highest)
    result = (inner_part + carried + d_skip[None, :, None] * values).reshape(row_count, DI)
    gated_rows = result * jax.nn.silu(gate_part)
    inv_scale = lax.rsqrt(lax.optimization_barrier(jnp.mean(gated_rows * gated_rows, axis=-1, keepdims=True)) + epsilon)
    return gated_rows * inv_scale * gain_out[None, :]

def mid_sequence(projected, conv_weight, conv_bias, dt_bias, a_log, d_skip, gain_out):
    state_now = jnp.zeros((H, P_SIZE, STATE), jnp.float32)
    halo_rows = jnp.zeros((KCONV - 1, CONV), jnp.float32)
    outputs = []
    for start in range(0, LENGTH, GROUP):
        block = projected[start:start + GROUP]
        pieces = split_conv(block, halo_rows, conv_weight, conv_bias, dt_bias, a_log)
        outputs.append(group_output(*pieces, state_now, d_skip, gain_out))
        state_now = jnp.exp(pieces[4][-1])[:, None, None] * state_now + group_state(pieces[0], pieces[1], pieces[3], pieces[4])
        halo_rows = block[GROUP - (KCONV - 1):, DI:DI + CONV]
    return jnp.concatenate(outputs, axis=0)

def layer_forward(rows, w_in, w_out, params):
    inv_scale = lax.rsqrt(lax.optimization_barrier(jnp.mean(rows * rows, axis=-1, keepdims=True)) + epsilon)
    normed = (rows * inv_scale * params[0][None, :]).astype(jnp.bfloat16)
    projected = jnp.dot(normed, w_in, preferred_element_type=jnp.float32)
    mixed_rows = mid_sequence(projected, *params[1:])
    rounded = mixed_rows.astype(jnp.bfloat16)
    return rows + jnp.dot(rounded, w_out.T, preferred_element_type=jnp.float32)

def layer_backward(rows, grad_rows, w_in, w_out, params):
    inv_scale = lax.rsqrt(lax.optimization_barrier(jnp.mean(rows * rows, axis=-1, keepdims=True)) + epsilon)
    plain_rows = rows * inv_scale
    normed = (plain_rows * params[0][None, :]).astype(jnp.bfloat16)
    projected = jnp.dot(normed, w_in, preferred_element_type=jnp.float32)
    mixed_rows, pull_back = jax.vjp(mid_sequence, projected, *params[1:])
    rounded = mixed_rows.astype(jnp.bfloat16)
    grad_bf = grad_rows.astype(jnp.bfloat16)
    out_w_grad = jnp.dot(grad_bf.T, rounded, preferred_element_type=jnp.float32)
    d_mixed = jnp.dot(grad_bf, w_out, preferred_element_type=jnp.float32)
    pulled = pull_back(d_mixed)
    proj_bf = pulled[0].astype(jnp.bfloat16)
    in_w_grad = jnp.dot(normed.T, proj_bf, preferred_element_type=jnp.float32)
    d_normed = jnp.dot(proj_bf, w_in.T, preferred_element_type=jnp.float32)
    gain_grad = lax.optimization_barrier(jnp.sum(d_normed * plain_rows, axis=0))
    d_plain = d_normed * params[0][None, :]
    d_rows = inv_scale * (d_plain - plain_rows * lax.optimization_barrier(jnp.mean(d_plain * plain_rows, axis=-1, keepdims=True)))
    return (grad_rows + d_rows, (in_w_grad, out_w_grad, gain_grad) + tuple(pulled[1:]))

def run_forward(rows_all, w_in, w_out, params):
    sequences = rows_all.reshape(SEQS, LENGTH, D)
    result = lax.map(lambda seq_rows: layer_forward(seq_rows, w_in, w_out, params), sequences)
    return result.reshape(TOKENS, D)

def run_backward(rows_all, grad_all, w_in, w_out, params):

    def one_sequence(carry_sums, operands):
        seq_rows, seq_grads = operands
        grad_in, parts = layer_backward(seq_rows, seq_grads, w_in, w_out, params)
        return (jax.tree.map(jnp.add, carry_sums, parts), grad_in)
    shapes = ((D, IN_ALL), (D, DI), (D,), (KCONV, CONV), (CONV,), (H,), (H,), (H,), (DI,))
    initial = tuple((jnp.zeros(shape_now, jnp.float32) for shape_now in shapes))
    sums, grads_in = lax.scan(one_sequence, initial, (rows_all.reshape(SEQS, LENGTH, D), grad_all.reshape(SEQS, LENGTH, D)))
    return (grads_in.reshape(TOKENS, D), sums)

def reference(block_input, out_grad, in_weight, out_weight, gain_in, conv_weight, conv_bias, dt_bias, a_log, d_skip, gain_out):
    small_all = (gain_in, conv_weight, conv_bias, dt_bias, a_log, d_skip, gain_out)

    def layer_params(index):
        return tuple((parameter[index] for parameter in small_all))
    first_out = run_forward(block_input, in_weight[0], out_weight[0], layer_params(0))
    second_out = run_forward(first_out, in_weight[1], out_weight[1], layer_params(1))
    second_grad, second_sums = run_backward(first_out, out_grad, in_weight[1], out_weight[1], layer_params(1))
    first_grad, first_sums = run_backward(block_input, second_grad, in_weight[0], out_weight[0], layer_params(0))
    stacked = tuple((jnp.stack([first_sum, second_sum]) for first_sum, second_sum in zip(first_sums, second_sums)))
    return (jnp.stack([first_out, second_out]), jnp.stack([first_grad, second_grad]), stacked[0], stacked[1], stacked[2], stacked[3], stacked[4], stacked[5], stacked[6], stacked[7], stacked[8])
```

```python
import jax
import jax.numpy as jnp
from jax import lax
from jax.sharding import PartitionSpec as P

DI = 2048
H = 32
P_SIZE = 64
STATE = 128
KCONV = 4
GROUP = 128
LENGTH = 256
CONV = 2304


epsilon = 1e-05
highest = lax.Precision.DEFAULT


def from_behind(value, axis, steps):
    count = lax.axis_size(axis)
    first, last = (max(0, -steps), min(count, count - steps))
    return lax.ppermute(value, axis, [(source, source + steps) for source in range(first, last)])


def split_conv(gate_part, rest, halo_rows, conv_weight, conv_bias, dt_bias, a_log):
    row_count = rest.shape[0]
    raw_part = rest[:, :CONV]
    dt_raw = rest[:, CONV:]
    padded = jnp.concatenate([halo_rows, raw_part], axis=0)
    summed = conv_bias[None, :] + conv_weight[0][None, :] * padded[0:row_count]
    for offset in range(1, KCONV):
        summed = summed + conv_weight[offset][None, :] * padded[offset : offset + row_count]
    mixed_rows = jax.nn.silu(summed)
    values = mixed_rows[:, :DI].reshape(row_count, H, P_SIZE)
    b_input = mixed_rows[:, DI : DI + STATE]
    c_output = mixed_rows[:, DI + STATE :]
    step_size = jax.nn.softplus(dt_raw + dt_bias[None, :])
    cumulative = jnp.cumsum(step_size * (-jnp.exp(a_log))[None, :], axis=0)
    return (values, b_input, c_output, step_size, cumulative, gate_part)


def group_state(values, b_input, step_size, cumulative):
    weight = jnp.exp(cumulative[-1:, :] - cumulative) * step_size
    return jnp.einsum("sh,shp,sn->hpn", weight, values, b_input, precision=highest)


def group_output(
    values, b_input, c_output, step_size, cumulative, gate_part, state_in, d_skip, gain_out
):
    row_count = values.shape[0]
    scores = jnp.dot(c_output, b_input.T, precision=highest)
    causal_mask = (jnp.arange(row_count)[:, None] >= jnp.arange(row_count)[None, :])[None, :, :]
    cum_heads = cumulative.T
    log_gap = cum_heads[:, :, None] - cum_heads[:, None, :]
    decays = jnp.where(causal_mask, jnp.exp(jnp.where(causal_mask, log_gap, 0.0)), 0.0)
    mixing = scores[None, :, :] * decays * step_size.T[:, None, :]
    inner_part = jnp.einsum("hts,shp->thp", mixing, values, precision=highest)
    carried = jnp.exp(cumulative)[:, :, None] * jnp.einsum(
        "tn,hpn->thp", c_output, state_in, precision=highest
    )
    result = (inner_part + carried + d_skip[None, :, None] * values).reshape(row_count, DI)
    gated_rows = result * jax.nn.silu(gate_part)
    inv_scale = lax.rsqrt(jnp.mean(gated_rows * gated_rows, axis=-1, keepdims=True) + epsilon)
    return gated_rows * inv_scale * gain_out[None, :]


def mid_sequence(gate_all, rest_all, conv_weight, conv_bias, dt_bias, a_log, d_skip, gain_out):
    state_now = jnp.zeros((H, P_SIZE, STATE), jnp.float32)
    halo_rows = jnp.zeros((KCONV - 1, CONV), jnp.float32)
    outputs = []
    for start in range(0, LENGTH, GROUP):
        gate_part = gate_all[start : start + GROUP]
        block = rest_all[start : start + GROUP]
        pieces = split_conv(gate_part, block, halo_rows, conv_weight, conv_bias, dt_bias, a_log)
        outputs.append(group_output(*pieces, state_now, d_skip, gain_out))
        if start + GROUP < LENGTH:
            state_now = jnp.exp(pieces[4][-1])[:, None, None] * state_now + group_state(
                pieces[0], pieces[1], pieces[3], pieces[4]
            )
            halo_rows = block[GROUP - (KCONV - 1) :, :CONV]
    return jnp.concatenate(outputs, axis=0)


def project(rows, gain, w_gate, w_rest):
    inv_scale = lax.rsqrt(jnp.mean(rows * rows, axis=-1, keepdims=True) + epsilon)
    plain_rows = rows * inv_scale
    normed = (plain_rows * gain[None, :]).astype(jnp.bfloat16)
    rest = jnp.dot(normed, w_rest, preferred_element_type=jnp.float32)
    gate = jnp.dot(normed, w_gate, preferred_element_type=jnp.float32)
    return (inv_scale, plain_rows, normed, gate, rest)


def finish(rows, mixed_rows, w_out):
    rounded = mixed_rows.astype(jnp.bfloat16)
    output = rows + jnp.einsum("ti,di->td", rounded, w_out, preferred_element_type=jnp.float32)
    return (output, rounded)


def back_rows(grad_rows, d_gate, d_rest, inv_scale, plain_rows, gain, w_gate, w_rest):
    d_normed = jnp.einsum(
        "tj,dj->td", d_gate.astype(jnp.bfloat16), w_gate, preferred_element_type=jnp.float32
    ) + jnp.einsum(
        "tj,dj->td", d_rest.astype(jnp.bfloat16), w_rest, preferred_element_type=jnp.float32
    )
    d_plain = d_normed * gain[None, :]
    d_rows = inv_scale * (
        d_plain - plain_rows * jnp.mean(d_plain * plain_rows, axis=-1, keepdims=True)
    )
    return (grad_rows + d_rows, jnp.sum(d_normed * plain_rows, axis=0))


def scatter_sum(partial):
    return lax.psum_scatter(
        partial.astype(jnp.bfloat16), "dp", scatter_dimension=0, tiled=True
    ).astype(jnp.float32)


def on_device(
    block_input,
    out_grad,
    in_weight,
    out_weight,
    gain_in,
    conv_weight,
    conv_bias,
    dt_bias,
    a_log,
    d_skip,
    gain_out,
):
    first_section = lax.axis_index("section") == 0
    params = tuple(
        (
            parameter[0]
            for parameter in (gain_in, conv_weight, conv_bias, dt_bias, a_log, d_skip, gain_out)
        )
    )
    gain = params[0]
    w_rest = lax.all_gather(in_weight[0, :, DI:], "dp", axis=0, tiled=True)
    w_gate = lax.all_gather(in_weight[0, :, :DI], "dp", axis=0, tiled=True)
    w_out = lax.all_gather(out_weight[0], "dp", axis=0, tiled=True)

    _, _, _, gate, rest = project(block_input, gain, w_gate, w_rest)
    mixed_rows = mid_sequence(gate, rest, *params[1:])
    out_first, _ = finish(block_input, mixed_rows, w_out)
    arrived = from_behind(out_first.astype(jnp.bfloat16), "section", 1)
    rows = jnp.where(first_section, block_input, arrived.astype(jnp.float32))

    inv_scale, plain_rows, normed, gate, rest = project(rows, gain, w_gate, w_rest)
    mixed_rows, pull_back = jax.vjp(mid_sequence, gate, rest, *params[1:])
    output, rounded = finish(rows, mixed_rows, w_out)

    def pull(grad_bf):
        d_mixed = jnp.dot(grad_bf, w_out, preferred_element_type=jnp.float32)
        return pull_back(d_mixed)

    pulled = pull(out_grad.astype(jnp.bfloat16))
    grad_second, _ = back_rows(
        out_grad, pulled[0], pulled[1], inv_scale, plain_rows, gain, w_gate, w_rest
    )
    returned = from_behind(grad_second.astype(jnp.bfloat16), "section", -1)
    grad_rows = jnp.where(first_section, returned.astype(jnp.float32), out_grad)
    grad_bf = grad_rows.astype(jnp.bfloat16)
    out_w_grad = jnp.einsum("td,ti->di", grad_bf, rounded, preferred_element_type=jnp.float32)
    out_grad_own = scatter_sum(out_w_grad)
    pulled = pull(grad_bf)
    grad_total, gain_grad = back_rows(
        grad_rows, pulled[0], pulled[1], inv_scale, plain_rows, gain, w_gate, w_rest
    )
    in_grad_own = jnp.concatenate(
        [
            scatter_sum(
                jnp.einsum(
                    "td,tj->dj",
                    normed,
                    part.astype(jnp.bfloat16),
                    preferred_element_type=jnp.float32,
                )
            )
            for part in pulled[:2]
        ],
        axis=1,
    )
    small = (gain_grad,) + tuple(pulled[2:])
    packed = lax.psum(jnp.concatenate([part.reshape(-1) for part in small]), "dp")
    small_sums = []
    start = 0
    for part in small:
        small_sums.append(packed[start : start + part.size].reshape(part.shape))
        start += part.size
    return (output[None], grad_total[None], in_grad_own[None], out_grad_own[None]) + tuple(
        (summed_grad[None] for summed_grad in small_sums)
    )


def solution(mesh):
    return jax.shard_map(
        on_device,
        mesh=mesh,
        in_specs=(
            P("dp", None),
            P("dp", None),
            P("section", "dp", None),
            P("section", "dp", None),
            P("section", None),
            P("section", None, None),
            P("section", None),
            P("section", None),
            P("section", None),
            P("section", None),
            P("section", None),
        ),
        out_specs=(
            P("section", "dp", None),
            P("section", "dp", None),
            P("section", "dp", None),
            P("section", "dp", None),
            P("section", None),
            P("section", None, None),
            P("section", None),
            P("section", None),
            P("section", None),
            P("section", None),
            P("section", None),
        ),
        check_vma=False,
    )
```

```python
import jax
import jax.numpy as jnp
from jax import lax
from jax.experimental import pallas as pl
from jax.experimental.pallas import tpu as pltpu
from jax.sharding import PartitionSpec as P

DI = 2048
H = 32
P_SIZE = 64
STATE = 128
KCONV = 4
GROUP = 128
LENGTH = 256
CONV = 2304
LANES = 128
PAIRS = DI // LANES
BLOCKS = LENGTH // GROUP

epsilon = 1e-05
highest = lax.Precision.HIGHEST
f32 = jnp.float32
bf16 = jnp.bfloat16


def from_behind(value, axis, steps):
    count = lax.axis_size(axis)
    first, last = (max(0, -steps), min(count, count - steps))
    return lax.ppermute(value, axis, [(source, source + steps) for source in range(first, last)])


def product(left, right, left_dim, right_dim, precision=None):
    return lax.dot_general(
        left,
        right,
        (((left_dim,), (right_dim,)), ((), ())),
        precision=precision,
        preferred_element_type=f32,
    )


def later(value, steps):
    if steps == 0:
        return value
    row = lax.broadcasted_iota(jnp.int32, value.shape, 0)
    return jnp.where(row >= steps, pltpu.roll(value, steps, axis=0), 0.0)


def earlier(value, steps):
    if steps == 0:
        return value
    count = value.shape[0]
    row = lax.broadcasted_iota(jnp.int32, value.shape, 0)
    return jnp.where(row < count - steps, pltpu.roll(value, count - steps, axis=0), 0.0)


def sigmoid(value):
    return 1.0 / (1.0 + jnp.exp(-value))


def silu_slope(value):
    gate = sigmoid(value)
    return gate * (1.0 + value * (1.0 - gate))


def convolve(raw, par):
    summed = par[KCONV : KCONV + 1] + par[0:1] * later(raw, KCONV - 1)
    for tap in range(1, KCONV):
        summed = summed + par[tap : tap + 1] * later(raw, KCONV - 1 - tap)
    return summed


def convolve_back(raw, d_summed, par):
    d_raw = par[0:1] * earlier(d_summed, KCONV - 1)
    rows = [jnp.sum(d_summed * later(raw, KCONV - 1), axis=0, keepdims=True)]
    for tap in range(1, KCONV):
        d_raw = d_raw + par[tap : tap + 1] * earlier(d_summed, KCONV - 1 - tap)
        rows.append(jnp.sum(d_summed * later(raw, KCONV - 1 - tap), axis=0, keepdims=True))
    rows.append(jnp.sum(d_summed, axis=0, keepdims=True))
    return d_raw, rows


def spread(row):
    return jnp.broadcast_to(row, (GROUP, GROUP))


def upright(row):
    return spread(row).T


def pair_decay(cum_pair, step_pair, scores):
    shape = (2 * GROUP, GROUP)
    tall = jnp.concatenate([upright(row) for row in cum_pair], axis=0)
    wide = jnp.concatenate([spread(row) for row in cum_pair], axis=0)
    steps = jnp.concatenate([spread(row) for row in step_pair], axis=0)
    here = lax.rem(lax.broadcasted_iota(jnp.int32, shape, 0), GROUP)
    there = lax.broadcasted_iota(jnp.int32, shape, 1)
    decay = jnp.where(here >= there, jnp.exp(jnp.where(here >= there, tall - wide, 0.0)), 0.0)
    both = jnp.concatenate([scores, scores], axis=0)
    return tall, decay, steps, both


def pair_weight(cum_pair, step_pair, low):
    rest = [jnp.exp(row[:, GROUP - 1 : GROUP] - row) for row in cum_pair]
    weights = [gap * step for gap, step in zip(rest, step_pair)]
    return rest, weights, jnp.where(low, upright(weights[0]), upright(weights[1]))


def block_rows(block):
    return slice(block * GROUP, (block + 1) * GROUP)


def low_lanes():
    return lax.broadcasted_iota(jnp.int32, (GROUP, LANES), 1) < P_SIZE


def triangle(lower):
    row = lax.broadcasted_iota(jnp.int32, (GROUP, GROUP), 0)
    column = lax.broadcasted_iota(jnp.int32, (GROUP, GROUP), 1)
    return jnp.where(row >= column if lower else row <= column, 1.0, 0.0).astype(f32)


def pair_rows(ref, pair, block):
    return [ref[pair, head : head + 1, block_rows(block)] for head in range(2)]


def all_rows(ref):
    return jnp.concatenate([ref[pair, 0:2, :] for pair in range(PAIRS)], axis=0)


def lanes_at(start, pair):
    return pl.ds(pl.multiple_of(start + pair * LANES, LANES), LANES)


def forward_kernel(
    proj, par, par_bc, heads, out, y_out, step_out, cum_out, b_keep, c_keep, score_keep, gated, squares
):
    pair = pl.program_id(0)

    @pl.when(pair == 0)
    def _():
        summed = convolve(proj[:, 2 * DI : DI + CONV], par_bc[...])
        mixed = summed * sigmoid(summed)
        b_all, c_all = mixed[:, :STATE], mixed[:, STATE:]
        b_keep[...] = b_all.astype(bf16)
        c_keep[...] = c_all.astype(bf16)
        raw_dt = proj[:, DI + CONV :]
        raw_dt = jnp.concatenate([raw_dt, jnp.zeros((LENGTH, LANES - H), f32)], axis=1).T[:H]
        raw_dt = raw_dt + heads[:, 0:1]
        step = jnp.maximum(raw_dt, 0.0) + jnp.log1p(jnp.exp(-jnp.abs(raw_dt)))
        scaled = step * heads[:, 1:2]
        for block in range(BLOCKS):
            at = block_rows(block)
            cum = product(scaled[:, at], triangle(False), 1, 0, highest)
            for other in range(PAIRS):
                cum_out[other, 0:2, at] = cum[2 * other : 2 * other + 2]
                step_out[other, 0:2, at] = step[2 * other : 2 * other + 2, at]
            score_keep[block] = product(c_all[at], b_all[at], 1, 1, highest)
        squares[...] = jnp.zeros_like(squares)

    low = low_lanes()
    here = lanes_at(0, pair)
    own = par[:, here]
    summed = convolve(proj[:, lanes_at(DI, pair)], own)
    values = summed * sigmoid(summed)
    gate = proj[:, here]
    state = None
    for block in range(BLOCKS):
        at = block_rows(block)
        cum_pair = pair_rows(cum_out, pair, block)
        step_pair = pair_rows(step_out, pair, block)
        tall, decay, steps, both = pair_decay(cum_pair, step_pair, score_keep[block])
        mixing = (both * decay * steps).astype(bf16)
        part = product(mixing, values[at].astype(bf16), 1, 0)
        y = jnp.where(low, part[:GROUP], part[GROUP:]) + own[6:7] * values[at]
        if block > 0:
            reach = jnp.exp(jnp.where(low, tall[:GROUP], tall[GROUP:]))
            y = y + reach * product(c_keep[at], state, 1, 1)
        else:
            _, _, weight = pair_weight(cum_pair, step_pair, low)
            state = product((values[at] * weight).astype(bf16), b_keep[at], 0, 0).astype(bf16)
        y_out[at, here] = y
        rows = y * gate[at] * sigmoid(gate[at])
        gated[pair, at] = rows
        squares[at] += rows * rows

    @pl.when(pair == PAIRS - 1)
    def _():
        mean = jnp.sum(squares[...], axis=1, keepdims=True) / DI
        inv = lax.rsqrt(mean + epsilon)
        for other in range(PAIRS):
            at = slice(other * LANES, (other + 1) * LANES)
            out[:, at] = (gated[other] * inv * par[5:6, at]).astype(bf16)


def backward_kernel(
    proj,
    y_in,
    d_out,
    step_in,
    cum_in,
    par,
    par_bc,
    heads,
    d_proj,
    sums,
    sums_bc,
    sums_heads,
    b_keep,
    c_keep,
    score_keep,
    d_score,
    d_b,
    d_c,
    inv_keep,
    pull_keep,
    d_cum,
    d_step,
):
    pair = pl.program_id(0)

    @pl.when(pair == 0)
    def _():
        summed = convolve(proj[:, 2 * DI : DI + CONV], par_bc[...])
        mixed = summed * sigmoid(summed)
        b_keep[...] = mixed[:, :STATE]
        c_keep[...] = mixed[:, STATE:]
        for block in range(BLOCKS):
            at = block_rows(block)
            score_keep[block] = product(c_keep[at], b_keep[at], 1, 1, highest)
        d_score[...] = jnp.zeros_like(d_score)
        d_b[...] = jnp.zeros_like(d_b)
        d_c[...] = jnp.zeros_like(d_c)

        def add_lanes(other, carried):
            square, pull = carried
            here = lanes_at(0, other)
            gate = proj[:, here]
            rows = y_in[:, here] * gate * sigmoid(gate)
            return (square + rows * rows, pull + d_out[:, here] * par[5:6, here] * rows)

        nothing = jnp.zeros((LENGTH, LANES), f32)
        square, pull = lax.fori_loop(0, PAIRS, add_lanes, (nothing, nothing))
        inv = lax.rsqrt(jnp.sum(square, axis=1, keepdims=True) / DI + epsilon)
        pull = jnp.sum(pull, axis=1, keepdims=True) / DI * inv * inv * inv
        inv_keep[...] = jnp.broadcast_to(inv, (LENGTH, LANES))
        pull_keep[...] = jnp.broadcast_to(pull, (LENGTH, LANES))

    low = low_lanes()
    here = lanes_at(0, pair)
    own = par[:, here]
    raw = proj[:, lanes_at(DI, pair)]
    summed = convolve(raw, own)
    values = summed * sigmoid(summed)
    gate = proj[:, here]
    gate_sig = sigmoid(gate)
    gate_silu = gate * gate_sig
    y = y_in[:, here]
    rows = y * gate_silu
    inv = inv_keep[...]
    above = d_out[:, here]
    d_gain = jnp.sum(above * rows * inv, axis=0, keepdims=True)
    d_rows = inv * above * own[5:6] - rows * pull_keep[...]
    d_y = d_rows * gate_silu
    d_gate = d_rows * y * gate_sig * (1.0 + gate * (1.0 - gate_sig))
    d_proj[:, here] = d_gate.astype(bf16)

    first = block_rows(0)
    rest, weights, weight = pair_weight(
        pair_rows(cum_in, pair, 0), pair_rows(step_in, pair, 0), low
    )
    weighted = (values[first] * weight).astype(bf16)
    state = product(weighted, b_keep[first].astype(bf16), 0, 0).astype(bf16)
    d_state = None
    d_values = [None] * BLOCKS
    last_lane = lax.broadcasted_iota(jnp.int32, (1, GROUP), 1) == GROUP - 1
    for block in reversed(range(BLOCKS)):
        at = block_rows(block)
        cum_pair = pair_rows(cum_in, pair, block)
        step_pair = pair_rows(step_in, pair, block)
        tall, decay, steps, both = pair_decay(cum_pair, step_pair, score_keep[block])
        mixing = (both * decay * steps).astype(bf16)
        d_here = d_y[at]
        stacked = jnp.concatenate(
            [jnp.where(low, d_here, 0.0), jnp.where(low, 0.0, d_here)], axis=0
        ).astype(bf16)
        d_mixing = product(stacked, values[at].astype(bf16), 1, 1)
        d_x = product(mixing, stacked, 0, 0) + own[6:7] * d_here
        faded = d_mixing * decay
        d_decay = faded * both
        to_score = faded * steps
        d_score[block] += to_score[:GROUP] + to_score[GROUP:]
        d_gap = d_decay * steps
        step_rows = [
            jnp.sum(d_decay[head * GROUP : (head + 1) * GROUP], axis=0, keepdims=True)
            for head in range(2)
        ]
        cum_rows = []
        for head in range(2):
            one = d_gap[head * GROUP : (head + 1) * GROUP]
            cum_rows.append(jnp.sum(one.T - one, axis=0, keepdims=True))
        if block > 0:
            reach = jnp.exp(jnp.where(low, tall[:GROUP], tall[GROUP:]))
            d_carried = reach * d_here
            c_now = c_keep[at].astype(bf16)
            through = (d_carried * product(c_now, state, 1, 1)).T
            d_carried = d_carried.astype(bf16)
            d_state = product(d_carried, c_now, 0, 0).astype(bf16)
            d_c[at] += product(d_carried, state, 1, 0)
            for head in range(2):
                part = through[head * P_SIZE : (head + 1) * P_SIZE]
                cum_rows[head] += jnp.sum(part, axis=0, keepdims=True)
        else:
            d_weighted = product(b_keep[at].astype(bf16), d_state, 1, 1)
            d_x = d_x + d_weighted * weight
            d_b[at] += product(weighted, d_state, 1, 0)
            through = (d_weighted * values[at]).T
            for head in range(2):
                part = through[head * P_SIZE : (head + 1) * P_SIZE]
                d_weight = jnp.sum(part, axis=0, keepdims=True)
                step_rows[head] += d_weight * rest[head]
                moved = d_weight * weights[head]
                total = jnp.sum(moved, axis=1, keepdims=True)
                cum_rows[head] += jnp.where(last_lane, total, 0.0) - moved
        for head in range(2):
            d_step[pair, head : head + 1, at] = step_rows[head]
            d_cum[pair, head : head + 1, at] = cum_rows[head]
        d_values[block] = d_x
    d_summed = jnp.concatenate(d_values, axis=0) * silu_slope(summed)
    d_raw, rows_out = convolve_back(raw, d_summed, own)
    d_proj[:, lanes_at(DI, pair)] = d_raw.astype(bf16)
    d_skip = jnp.sum(d_y * values, axis=0, keepdims=True)
    sums[...] = jnp.concatenate(rows_out + [d_gain, d_skip, jnp.zeros_like(d_gain)], axis=0)

    @pl.when(pair == PAIRS - 1)
    def _():
        for block in range(BLOCKS):
            at = block_rows(block)
            d_c[at] += product(d_score[block], b_keep[at], 1, 0, highest)
            d_b[at] += product(d_score[block], c_keep[at], 0, 0, highest)
        raw_bc = proj[:, 2 * DI : DI + CONV]
        summed = convolve(raw_bc, par_bc[...])
        d_mixed = jnp.concatenate([d_b[...], d_c[...]], axis=1)
        d_raw, rows_out = convolve_back(raw_bc, d_mixed * silu_slope(summed), par_bc[...])
        d_proj[:, 2 * DI : DI + CONV] = d_raw.astype(bf16)
        sums_bc[...] = jnp.concatenate(
            rows_out + [jnp.zeros_like(rows_out[0])] * (8 - len(rows_out)), axis=0
        )
        raw_dt = proj[:, DI + CONV :]
        raw_dt = jnp.concatenate([raw_dt, jnp.zeros((LENGTH, LANES - H), f32)], axis=1).T[:H]
        slope = sigmoid(raw_dt + heads[:, 0:1])
        cum_all = all_rows(d_cum)
        d_scaled = jnp.concatenate(
            [
                product(cum_all[:, block_rows(block)], triangle(True), 1, 0, highest)
                for block in range(BLOCKS)
            ],
            axis=1,
        )
        d_dt = (all_rows(d_step) + d_scaled * heads[:, 1:2]) * slope
        rate = jnp.sum(d_scaled * all_rows(step_in), axis=1, keepdims=True) * heads[:, 1:2]
        bias = jnp.sum(d_dt, axis=1, keepdims=True)
        lane = lax.broadcasted_iota(jnp.int32, (H, LANES), 1)
        sums_heads[...] = jnp.where(lane == 0, bias, jnp.where(lane == 1, rate, 0.0))
        turned = jnp.concatenate([d_dt, jnp.zeros((LANES - H, LENGTH), f32)], axis=0).T
        d_proj[:, DI + CONV :] = turned[:, :H].astype(bf16)


def whole(shape):
    return pl.BlockSpec(shape, lambda pair: (0,) * len(shape))


def run_kernel(kernel, operands, results, result_specs, scratch, cost):
    return pl.pallas_call(
        kernel,
        grid=(PAIRS,),
        in_specs=[whole(operand.shape) for operand in operands],
        out_specs=result_specs,
        out_shape=results,
        scratch_shapes=scratch,
        cost_estimate=cost,
        compiler_params=pltpu.CompilerParams(
            dimension_semantics=("arbitrary",), vmem_limit_bytes=48 * 1024 * 1024
        ),
    )(*operands)


def scan_forward(projected, tables):
    shapes = [((LENGTH, DI), bf16), ((LENGTH, DI), f32), ((PAIRS, 8, LENGTH), f32), ((PAIRS, 8, LENGTH), f32)]
    return run_kernel(
        forward_kernel,
        (projected,) + tables,
        [jax.ShapeDtypeStruct(shape, kind) for shape, kind in shapes],
        [whole(shape) for shape, _ in shapes],
        [
            pltpu.VMEM((LENGTH, STATE), bf16),
            pltpu.VMEM((LENGTH, STATE), bf16),
            pltpu.VMEM((BLOCKS, GROUP, GROUP), f32),
            pltpu.VMEM((PAIRS, LENGTH, LANES), f32),
            pltpu.VMEM((LENGTH, LANES), f32),
        ],
        pl.CostEstimate(flops=10**9, bytes_accessed=8 * 10**6, transcendentals=10**6),
    )


def scan_backward(projected, y, d_out, step, cum, tables):
    shapes = [
        (projected.shape, bf16),
        ((8, DI), f32),
        ((8, CONV - DI), f32),
        ((H, LANES), f32),
    ]
    specs = [whole(shape) for shape, _ in shapes]
    specs[1] = pl.BlockSpec((8, LANES), lambda pair: (0, pair))
    return run_kernel(
        backward_kernel,
        (projected, y, d_out, step, cum) + tables,
        [jax.ShapeDtypeStruct(shape, kind) for shape, kind in shapes],
        specs,
        [
            pltpu.VMEM((LENGTH, STATE), f32),
            pltpu.VMEM((LENGTH, STATE), f32),
            pltpu.VMEM((BLOCKS, GROUP, GROUP), f32),
            pltpu.VMEM((BLOCKS, GROUP, GROUP), f32),
            pltpu.VMEM((LENGTH, STATE), f32),
            pltpu.VMEM((LENGTH, STATE), f32),
            pltpu.VMEM((LENGTH, LANES), f32),
            pltpu.VMEM((LENGTH, LANES), f32),
            pltpu.VMEM((PAIRS, 8, LENGTH), f32),
            pltpu.VMEM((PAIRS, 8, LENGTH), f32),
        ],
        pl.CostEstimate(flops=4 * 10**9, bytes_accessed=12 * 10**6, transcendentals=10**6),
    )


def make_tables(conv_weight, conv_bias, dt_bias, a_log, d_skip, gain_out):
    taps = jnp.concatenate([conv_weight, conv_bias[None]], axis=0)
    wide = jnp.stack([gain_out, jnp.repeat(d_skip, P_SIZE), jnp.zeros_like(gain_out)])
    par = jnp.concatenate([taps[:, :DI], wide], axis=0)
    par_bc = jnp.pad(taps[:, DI:], ((0, 8 - KCONV - 1), (0, 0)))
    heads = jnp.pad(jnp.stack([dt_bias, -jnp.exp(a_log)], axis=1), ((0, 0), (0, LANES - 2)))
    return (par, par_bc, heads)


def project(rows, gain, w_in):
    inv_scale = lax.rsqrt(jnp.mean(rows * rows, axis=-1, keepdims=True) + epsilon)
    plain_rows = rows * inv_scale
    normed = (plain_rows * gain[None, :]).astype(bf16)
    return (inv_scale, plain_rows, normed, jnp.dot(normed, w_in, preferred_element_type=f32))


def finish(rows, rounded, w_out):
    return rows + jnp.einsum("ti,di->td", rounded, w_out, preferred_element_type=f32)


def back_rows(grad_rows, d_proj, inv_scale, plain_rows, gain, w_in):
    d_normed = jnp.einsum("tj,dj->td", d_proj, w_in, preferred_element_type=f32)
    d_plain = d_normed * gain[None, :]
    d_rows = inv_scale * (
        d_plain - plain_rows * jnp.mean(d_plain * plain_rows, axis=-1, keepdims=True)
    )
    return (grad_rows + d_rows, jnp.sum(d_normed * plain_rows, axis=0))


def scatter_sum(partial):
    return lax.psum_scatter(
        partial.astype(bf16), "dp", scatter_dimension=0, tiled=True
    ).astype(f32)


def on_device(
    block_input,
    out_grad,
    in_weight,
    out_weight,
    gain_in,
    conv_weight,
    conv_bias,
    dt_bias,
    a_log,
    d_skip,
    gain_out,
):
    first_section = lax.axis_index("section") == 0
    gain = gain_in[0]
    tables = make_tables(
        conv_weight[0], conv_bias[0], dt_bias[0], a_log[0], d_skip[0], gain_out[0]
    )
    w_in = lax.all_gather(in_weight[0], "dp", axis=0, tiled=True)
    w_out = lax.all_gather(out_weight[0], "dp", axis=0, tiled=True)

    projected = project(block_input, gain, w_in)[3]
    out_first = finish(block_input, scan_forward(projected, tables)[0], w_out)
    arrived = from_behind(out_first.astype(bf16), "section", 1)
    rows = jnp.where(first_section, block_input, arrived.astype(f32))

    inv_scale, plain_rows, normed, projected = project(rows, gain, w_in)
    rounded, y, step, cum = scan_forward(projected, tables)
    output = finish(rows, rounded, w_out)

    def pull(grad_bf):
        d_out = jnp.dot(grad_bf, w_out, preferred_element_type=f32)
        return scan_backward(projected, y, d_out, step, cum, tables)

    d_proj = pull(out_grad.astype(bf16))[0]
    grad_second, _ = back_rows(out_grad, d_proj, inv_scale, plain_rows, gain, w_in)
    returned = from_behind(grad_second.astype(bf16), "section", -1)
    grad_rows = jnp.where(first_section, returned.astype(f32), out_grad)
    grad_bf = grad_rows.astype(bf16)
    out_grad_own = scatter_sum(
        jnp.einsum("td,ti->di", grad_bf, rounded, preferred_element_type=f32)
    )
    d_proj, sums, sums_bc, sums_heads = pull(grad_bf)
    in_grad_own = scatter_sum(
        jnp.einsum("td,tj->dj", normed, d_proj, preferred_element_type=f32)
    )
    grad_total, gain_grad = back_rows(grad_rows, d_proj, inv_scale, plain_rows, gain, w_in)
    taps = jnp.concatenate([sums[: KCONV + 1], sums_bc[: KCONV + 1]], axis=1)
    small = (
        gain_grad,
        taps[:KCONV],
        taps[KCONV],
        sums_heads[:, 0],
        sums_heads[:, 1],
        jnp.sum(sums[6].reshape(H, P_SIZE), axis=1),
        sums[5],
    )
    packed = lax.psum(jnp.concatenate([part.reshape(-1) for part in small]), "dp")
    small_sums = []
    start = 0
    for part in small:
        small_sums.append(packed[start : start + part.size].reshape(part.shape))
        start += part.size
    return (output[None], grad_total[None], in_grad_own[None], out_grad_own[None]) + tuple(
        (summed_grad[None] for summed_grad in small_sums)
    )


def solution(mesh):
    return jax.shard_map(
        on_device,
        mesh=mesh,
        in_specs=(
            P("dp", None),
            P("dp", None),
            P("section", "dp", None),
            P("section", "dp", None),
            P("section", None),
            P("section", None, None),
            P("section", None),
            P("section", None),
            P("section", None),
            P("section", None),
            P("section", None),
        ),
        out_specs=(
            P("section", "dp", None),
            P("section", "dp", None),
            P("section", "dp", None),
            P("section", "dp", None),
            P("section", None),
            P("section", None, None),
            P("section", None),
            P("section", None),
            P("section", None),
            P("section", None),
            P("section", None),
        ),
        check_vma=False,
    )
```
